32 devices in a mesh: cells: 8 (over z, y), grp: 4 (over x, core).
Axes of the slice: x: 2, y: 2, z: 4, core: 2. Of those that a mesh axis runs over, the one named last changes fastest.
Arguments:
- coeffs: bfloat16 [512, 6144], P(('cells', 'grp')), may hold values from -6 to 6
- neighbours: int32 [512, 32], P(('cells', 'grp')), may hold values from 0 to 47
- counts: int32 [512], P(('cells', 'grp')), may hold values from 8 to 32
- boxes: int32 [512], P(('cells', 'grp')), may hold values from 0 to 7
- axial: bfloat16 [512, 32, 96], P(('cells', 'grp')), may hold values from -1 to 1
- rotations: bfloat16 [32, 96, 96], replicated, may hold values from -0.625 to 0.625
- out_map: bfloat16 [96, 96], replicated, may hold values from -0.625 to 0.625
- coupling: bfloat16 [64, 64], replicated, may hold values from -1 to 1, as said below
- in_map: bfloat16 [96, 96], replicated, may hold values from -0.21875 to 0.21875
- tmat: float32 [512, 96], P(('cells', 'grp')), may hold values from -0.5 to 0.5
Outputs:
- product: bfloat16 [512, 6144], P(('cells', 'grp'))
The draws below stay inside these ranges and needn't reach their ends.
Inputs may be any that keep to these rules, and one draw needn't show every extreme that they name: Entries of coupling are zero on the diagonal.
All inputs are finite; a program needn't handle non-finite values.
Results may differ from the reference program's by a relative error of at most 0.0043.
Values may be sent and summed in bfloat16 or wider, within the bound.
A program may use at most 64 MiB of HBM per device.

```python
import jax
import jax.numpy as jnp
from jax import lax

C = 96
P_SIZE = 64
K = 32
SD = 16
NBG = 2
NBC = 8
NBOX = 64
BOX_SPH = 8
S = 512
N_CELLS = 8
N_GRP = 4


def draw_coupling(key, part):
    values = jax.random.normal(key, (NBOX, NBOX), jnp.float32) * (2.0 / NBOX ** 0.5)
    values = jnp.clip(values, -1.0, 1.0)
    rows = jnp.arange(NBOX, dtype=jnp.int32)
    offdiag = (rows[:, None] != rows[None, :]).astype(jnp.float32)
    return (values * offdiag).astype(jnp.bfloat16)


def place_ends(entries, rng, least, largest):
    index_at = [jax.random.randint(jax.random.fold_in(rng, axis), (), 0, length) for axis, length in enumerate(entries.shape)]
    longest = entries.shape.index(max(entries.shape))
    next_to = index_at[:longest] + [(index_at[longest] + 1) % entries.shape[longest]] + index_at[longest + 1:]
    return entries.at[tuple(index_at)].set(least).at[tuple(next_to)].set(largest)


def levels(rng, shape, pieces, smallest, largest):
    factor_of, own = 1.0, jax.random.fold_in(rng, 6)
    for axis_at, parts in pieces:
        heights = jnp.exp(jax.random.uniform(jax.random.fold_in(own, axis_at), (parts,), jnp.float32, smallest / len(pieces), largest / len(pieces)))
        factor_of = factor_of * jnp.repeat(heights, shape[axis_at] // parts).reshape([-1 if axis == axis_at else 1 for axis in range(len(shape))])
    return factor_of


def gaussian(stream_key, extent, scale, reach, split=(), kind=jnp.bfloat16):
    result = jax.random.normal(stream_key, extent, jnp.float32) * scale
    if len(split) > 0:
        result = levels(stream_key, extent, split, -0.22, 0.18) * result
    return jnp.clip(result, min=-reach, max=reach).astype(kind)


def setup_inputs(seed: int = 0) -> dict:
    splits = jax.random.split(jax.random.key(seed), 11)
    return {
        "coeffs": gaussian(splits[0], (S, C * P_SIZE), 1.0, 6.0, ((0, 32),)),
        "neighbours": place_ends(jax.random.randint(splits[1], (S, K), 0, 3 * SD), jax.random.fold_in(splits[1], 1), 0, (3 * SD) - 1).astype(jnp.int32),
        "counts": place_ends(jax.random.randint(splits[2], (S,), K // 4, K + 1), jax.random.fold_in(splits[2], 1), K // 4, K).astype(jnp.int32),
        "boxes": place_ends(jax.random.randint(splits[3], (S,), 0, NBC), jax.random.fold_in(splits[3], 1), 0, NBC - 1).astype(jnp.int32),
        "axial": gaussian(splits[4], (S, K, C), 0.18, 1.0, ((0, 32),)),
        "rotations": gaussian(splits[5], (K, C, C), C ** -0.5, 0.625),
        "out_map": gaussian(splits[6], (C, C), C ** -0.5, 0.625),
        "coupling": draw_coupling(jax.random.fold_in(splits[10], 71), 0),
        "in_map": gaussian(splits[8], (C, C), (C * BOX_SPH) ** -0.5, 0.21875),
        "tmat": jnp.clip(jax.random.uniform(splits[9], (S, C), jnp.float32, -0.5, 0.5) * levels(splits[9], (S, C), ((0, 32),), -0.4, 0.0), -0.5, 0.5),
    }


slot_width = 8


def near_field(cand, nbr, cnt, axial, rot):
    sd, slots = nbr.shape
    width = rot.shape[1]
    incid = cand.shape[1] // width
    groups = slots // slot_width
    live = (lax.broadcasted_iota(jnp.int32, (sd, slots), 1) < cnt[:, None]).astype(jnp.float32)
    scale = axial.astype(jnp.float32) * live[:, :, None]
    idx_groups = nbr.reshape(sd, groups, slot_width).transpose(1, 0, 2)
    scale_groups = scale.reshape(sd, groups, slot_width, width).transpose(1, 0, 2, 3)
    rot_groups = rot.reshape(groups, slot_width, width, width)

    def step(total, item):
        idx, factor, rg = item
        picked = cand[idx].reshape(sd, slot_width, width, incid)
        rg32 = rg.astype(jnp.float32)
        turned = jnp.einsum('kdc,skcp->skdp', rg32, picked.astype(jnp.float32))
        scaled = (turned * factor[..., None]).astype(jnp.bfloat16)
        back = jnp.einsum('kdc,skdp->scp', rg32, scaled.astype(jnp.float32))
        return total + back, None

    start = jnp.zeros((sd, width, incid), jnp.float32)
    total, _ = lax.scan(step, start, (idx_groups, scale_groups, rot_groups))
    return total


def apply_tmat(field, tmat):
    half = field.shape[1] // 2
    real_t = tmat[:, :half, None]
    imag_t = tmat[:, half:, None]
    real_u = field[:, :half]
    imag_u = field[:, half:]
    return jnp.concatenate([real_t * real_u - imag_t * imag_u, real_t * imag_u + imag_t * real_u], axis=1)


def reference(coeffs, neighbours, counts, boxes, axial, rotations, out_map, coupling, in_map, tmat):
    ncell = N_CELLS
    ngrp = N_GRP
    total = coeffs.shape[0]
    blocks = ncell * ngrp
    sd = total // blocks
    width = rotations.shape[1]
    incid = coeffs.shape[1] // width
    nbc = NBG * ngrp
    x4 = coeffs.reshape(ncell, ngrp, sd, width * incid)
    zero = jnp.zeros((1, ngrp, sd, width * incid), jnp.bfloat16)
    before = jnp.concatenate([zero, x4[:-1]], axis=0)
    after = jnp.concatenate([x4[1:], zero], axis=0)
    cand = jnp.concatenate([before, x4, after], axis=2).reshape(blocks, 3 * sd, width * incid)

    def one_block(item):
        cb, nb, cn, ax = item
        return near_field(cb, nb, cn, ax, rotations)

    near = lax.map(one_block, (cand, neighbours.reshape(blocks, sd, -1), counts.reshape(blocks, sd),
                               axial.reshape(blocks, sd, -1, width)))
    near = near.reshape(total, width, incid)

    onehot = (boxes.reshape(ncell, ngrp * sd)[:, :, None] == jnp.arange(nbc, dtype=jnp.int32)[None, None, :]).astype(jnp.float32)
    xcol = coeffs.reshape(ncell, ngrp * sd, width * incid).astype(jnp.float32)
    sums = jnp.einsum('nsb,nsq->nbq', onehot, xcol, precision=lax.Precision.HIGHEST)
    sums = sums.reshape(ncell, nbc, width, incid)
    moments = jnp.einsum('dc,nbcp->nbdp', out_map.astype(jnp.float32), sums, precision=lax.Precision.HIGHEST).astype(jnp.bfloat16)
    moments = moments.reshape(ncell * nbc, width * incid)
    local = jnp.dot(coupling, moments, preferred_element_type=jnp.float32).astype(jnp.bfloat16)
    local = local.reshape(ncell, nbc, width * incid).astype(jnp.float32)
    chosen = jnp.einsum('nsb,nbq->nsq', onehot, local, precision=lax.Precision.HIGHEST)
    chosen = chosen.reshape(total, width, incid)
    far = jnp.einsum('dc,scp->sdp', in_map.astype(jnp.float32), chosen, precision=lax.Precision.HIGHEST)
    field = near + far
    turned = apply_tmat(field, tmat).reshape(total, width * incid)
    return (coeffs.astype(jnp.float32) - turned).astype(jnp.bfloat16)
```

```python
import functools

import jax
import jax.numpy as jnp
from jax import lax
from jax.experimental import pallas as pl
from jax.experimental.pallas import tpu as pltpu
from jax.sharding import PartitionSpec as P

NBG = 2
MESH = pl.DeviceIdType.MESH
F32 = jnp.float32
BF16 = jnp.bfloat16


def dot_nt(a, b):
    return lax.dot_general(a, b, (((1,), (1,)), ((), ())), preferred_element_type=F32)


def kernel(dims, nbr_ref, cnt_ref, box_ref, x_ref, axial_ref, rot_ref, out_map_ref, coup_ref, in_map_ref, tmat_ref,
           o_ref, cand, w_pair, w_stack, scale, acc, sums, part, arrived, mom, mall, lhs_c, loc, ball, farbuf, maps,
           h_send, h_recv, f_send, f_recv, a_send, a_recv, m_send, m_recv, l_send, l_recv):
    ncell, ngrp, chunks, sd, slots, width, incid, lanes, nbc, pq = dims
    half = width // 2
    rows = nbc * pq
    pairs = slots // 2
    n = lax.axis_index("cells")
    g = lax.axis_index("grp")
    par = n % 2
    partner = n + 1 - 2 * par
    onward = n + 2 - 4 * par
    source = n - 2 + 4 * par
    forwards = jnp.logical_and(onward >= 0, onward < ncell)
    receives = jnp.logical_and(source >= 0, source < ncell)
    near_slot = 2 * (1 - par)
    other_slot = 2 * par
    step = sd // chunks

    def cell(d):
        return lax.rem(n + d, ncell)

    def member(d):
        return lax.rem(g + d, ngrp)

    barrier = pltpu.get_barrier_semaphore()
    for d in range(1, ncell):
        pl.semaphore_signal(barrier, inc=1, device_id=(cell(d), g), device_id_type=MESH)
    for d in range(1, ngrp):
        pl.semaphore_signal(barrier, inc=1, device_id=(n, member(d)), device_id_type=MESH)
    pl.semaphore_wait(barrier, ncell + ngrp - 2)

    def swap(h):
        return pltpu.make_async_remote_copy(
            src_ref=x_ref.at[pl.ds(h * step, step)], dst_ref=cand.at[pl.ds(other_slot * sd + h * step, step)],
            send_sem=h_send.at[h], recv_sem=h_recv.at[h], device_id=(partner, g), device_id_type=MESH)

    def forward(h):
        return pltpu.make_async_remote_copy(
            src_ref=cand.at[pl.ds(near_slot * sd + h * step, step)],
            dst_ref=cand.at[pl.ds(other_slot * sd + h * step, step)],
            send_sem=f_send.at[h], recv_sem=f_recv.at[h], device_id=(onward, g), device_id_type=MESH)

    for h in range(chunks):
        swap(h).start()

    xs = [x_ref[s].astype(F32) for s in range(sd)]
    for b in range(nbc):
        total = None
        for s in range(sd):
            term = xs[s] * jnp.where(box_ref[s] == b, 1.0, 0.0)
            total = term if total is None else total + term
        for q in range(ngrp):
            sums[q, b * pq:(b + 1) * pq, :] = total[q * pq:(q + 1) * pq]
    for q in range(ngrp):
        part[q] = sums[q].astype(BF16)

    def spread(d):
        return pltpu.make_async_remote_copy(
            src_ref=part.at[member(d)], dst_ref=arrived.at[d], send_sem=a_send.at[d], recv_sem=a_recv.at[d],
            device_id=(n, member(d)), device_id_type=MESH)

    for d in range(1, ngrp):
        spread(d).start()

    cand[sd:2 * sd] = x_ref[...]

    @pl.when(jnp.logical_not(receives))
    def _():
        cand[pl.ds(other_slot * sd, sd)] = jnp.zeros((sd, incid, lanes), BF16)

    for m, ref in enumerate((out_map_ref, in_map_ref)):
        maps[m] = jnp.zeros((lanes, lanes), BF16)
        maps[m, :width, :width] = ref[...]

    for d in range(1, ngrp):
        spread(d).wait_recv()
    total = sums[g]
    for d in range(1, ngrp):
        total = total + arrived[d].astype(F32)
    moment = dot_nt(total.astype(BF16), maps[0]).astype(BF16)
    mom[...] = moment

    def share(d):
        return pltpu.make_async_remote_copy(
            src_ref=mom, dst_ref=mall.at[n], send_sem=m_send.at[d], recv_sem=m_recv.at[d],
            device_id=(cell(d), g), device_id_type=MESH)

    for d in range(1, ncell):
        share(d).start()
    mall[n] = moment

    for h in range(chunks):
        swap(h).wait_recv()

        @pl.when(forwards)
        def _():
            forward(h).start()

    w_pair[...] = jnp.zeros_like(w_pair)
    w_stack[...] = jnp.zeros_like(w_stack)
    scale[...] = jnp.zeros_like(scale)
    acc[...] = jnp.zeros_like(acc)

    @pl.loop(0, pairs)
    def _(j):
        for i in range(2):
            r = rot_ref[2 * j + i]
            w_pair[j, i * lanes:i * lanes + width, i * lanes:i * lanes + width] = r
            w_stack[j, i * lanes:i * lanes + width, :width] = r

    slot_id = lax.broadcasted_iota(jnp.int32, (slots, width), 0)
    for s in range(sd):
        live = jnp.where(slot_id < cnt_ref[s], 1.0, 0.0)
        scale[s, :, :width] = axial_ref[s].astype(F32) * live

    nbox = ncell * nbc
    row_box = lax.broadcasted_iota(jnp.int32, (rows, nbox), 0) // pq + n * nbc
    pick = (row_box == lax.broadcasted_iota(jnp.int32, (rows, nbox), 1)).astype(F32).astype(BF16)
    mine = jnp.dot(pick, coup_ref[...], preferred_element_type=F32).astype(BF16)
    for c in range(ncell):
        col_box = lax.broadcasted_iota(jnp.int32, (nbox, rows), 1) // pq + c * nbc
        put = (col_box == lax.broadcasted_iota(jnp.int32, (nbox, rows), 0)).astype(F32).astype(BF16)
        wide = jnp.dot(mine, put, preferred_element_type=F32)
        same = (lax.broadcasted_iota(jnp.int32, (rows, rows), 0) % pq
                == lax.broadcasted_iota(jnp.int32, (rows, rows), 1) % pq)
        lhs_c[c] = jnp.where(same, wide, 0.0).astype(BF16)

    @pl.when(receives)
    def _():
        for h in range(chunks):
            forward(h).wait_recv()

    block = 4

    def near(j):
        for sb in range(0, sd, block):
            lhs = jnp.concatenate([
                jnp.concatenate([cand[nbr_ref[s, 2 * j]], cand[nbr_ref[s, 2 * j + 1]]], axis=1)
                for s in range(sb, sb + block)], axis=0)
            turned = dot_nt(lhs, w_pair[j])
            scaled = jnp.concatenate([
                turned[(s - sb) * incid:(s - sb + 1) * incid]
                * jnp.concatenate([scale[s, pl.ds(2 * j, 1), :], scale[s, pl.ds(2 * j + 1, 1), :]], axis=1)
                for s in range(sb, sb + block)], axis=0).astype(BF16)
            acc[sb * incid:(sb + block) * incid, :] += jnp.dot(scaled, w_stack[j], preferred_element_type=F32)

    @pl.loop(0, pairs // 2)
    def _(j):
        near(j)

    for d in range(1, ncell):
        share(d).wait_recv()
    local = jnp.zeros((rows, lanes), F32)
    for c in range(ncell):
        local = local + jnp.dot(lhs_c[c], mall[c], preferred_element_type=F32)
    local = local.astype(BF16)
    loc[...] = local

    def spread_local(d):
        return pltpu.make_async_remote_copy(
            src_ref=loc, dst_ref=ball.at[g], send_sem=l_send.at[d], recv_sem=l_recv.at[d],
            device_id=(n, member(d)), device_id_type=MESH)

    for d in range(1, ngrp):
        spread_local(d).start()
    ball[g] = local

    @pl.loop(pairs // 2, pairs)
    def _(j):
        near(j)

    for d in range(1, ngrp):
        spread_local(d).wait_recv()
    for q in range(ngrp):
        far = dot_nt(ball[q], maps[1])
        for b in range(nbc):
            farbuf[b, q * pq:(q + 1) * pq, :] = far[b * pq:(b + 1) * pq]

    lane = lax.broadcasted_iota(jnp.int32, (incid, lanes), 1)
    fill = jnp.zeros((sd, lanes - width), F32)
    real_t = tmat_ref[:, :half]
    imag_t = tmat_ref[:, half:]
    same_t = jnp.concatenate([real_t, real_t, fill], axis=1)
    swap_t = jnp.concatenate([-imag_t, imag_t, fill], axis=1)
    for s in range(sd):
        u = acc[s * incid:(s + 1) * incid, :] + farbuf[box_ref[s]]
        turned = jnp.where(lane < half, pltpu.roll(u, lanes - half, 1), pltpu.roll(u, half, 1))
        v = same_t[s:s + 1] * u + swap_t[s:s + 1] * turned
        o_ref[s] = (x_ref[s].astype(F32) - v).astype(BF16)

    for h in range(chunks):
        swap(h).wait_send()

    @pl.when(forwards)
    def _():
        for h in range(chunks):
            forward(h).wait_send()

    for d in range(1, ngrp):
        spread(d).wait_send()
        spread_local(d).wait_send()
    for d in range(1, ncell):
        share(d).wait_send()


def shards(ncell, ngrp, coeffs, neighbours, counts, boxes, axial, rotations, out_map, coupling, in_map, tmat):
    sd, slots = neighbours.shape
    width = rotations.shape[1]
    incid = coeffs.shape[1] // width
    lanes = -(-width // 128) * 128
    nbc = NBG * ngrp
    pq = incid // ngrp
    rows = nbc * pq
    chunks = 4
    pairs = slots // 2
    x = jnp.pad(coeffs.reshape(sd, width, incid).transpose(0, 2, 1), ((0, 0), (0, 0), (0, lanes - width)))
    smem = pl.BlockSpec(memory_space=pltpu.SMEM)
    vmem = pl.BlockSpec(memory_space=pltpu.VMEM)
    dma = pltpu.SemaphoreType.DMA
    out = pl.pallas_call(
        functools.partial(kernel, (ncell, ngrp, chunks, sd, slots, width, incid, lanes, nbc, pq)),
        out_shape=jax.ShapeDtypeStruct((sd, incid, lanes), BF16),
        in_specs=[smem] * 3 + [vmem] * 7,
        out_specs=vmem,
        scratch_shapes=[
            pltpu.VMEM((3 * sd, incid, lanes), BF16),
            pltpu.VMEM((pairs, 2 * lanes, 2 * lanes), BF16),
            pltpu.VMEM((pairs, 2 * lanes, lanes), BF16),
            pltpu.VMEM((sd, slots, lanes), F32),
            pltpu.VMEM((sd * incid, lanes), F32),
            pltpu.VMEM((ngrp, rows, lanes), F32),
            pltpu.VMEM((ngrp, rows, lanes), BF16),
            pltpu.VMEM((ngrp, rows, lanes), BF16),
            pltpu.VMEM((rows, lanes), BF16),
            pltpu.VMEM((ncell, rows, lanes), BF16),
            pltpu.VMEM((ncell, rows, rows), BF16),
            pltpu.VMEM((rows, lanes), BF16),
            pltpu.VMEM((ngrp, rows, lanes), BF16),
            pltpu.VMEM((nbc, incid, lanes), F32),
            pltpu.VMEM((2, lanes, lanes), BF16),
            dma((chunks,)), dma((chunks,)), dma((chunks,)), dma((chunks,)),
            dma((ngrp,)), dma((ngrp,)), dma((ncell,)), dma((ncell,)), dma((ngrp,)), dma((ngrp,)),
        ],
        compiler_params=pltpu.CompilerParams(collective_id=0, has_side_effects=True),
    )(neighbours, counts, boxes, x, axial, rotations, out_map, coupling, in_map, tmat)
    return out[:, :, :width].transpose(0, 2, 1).reshape(sd, width * incid)


def solution(mesh):
    in_specs = (
        P(("cells", "grp"), None),
        P(("cells", "grp"), None),
        P(("cells", "grp")),
        P(("cells", "grp")),
        P(("cells", "grp"), None, None),
        P(),
        P(),
        P(),
        P(),
        P(("cells", "grp"), None),
    )
    out_specs = P(("cells", "grp"), None)
    body = functools.partial(shards, mesh.shape["cells"], mesh.shape["grp"])
    return jax.shard_map(body, mesh=mesh, in_specs=in_specs, out_specs=out_specs, check_vma=False)
```

```python
import functools

import jax
import jax.numpy as jnp
from jax import lax
from jax.experimental import pallas as pl
from jax.experimental.pallas import tpu as pltpu
from jax.sharding import PartitionSpec as P

NBG = 2
MESH = pl.DeviceIdType.MESH
F32 = jnp.float32
BF16 = jnp.bfloat16


def dot_nt(a, b):
    return lax.dot_general(a, b, (((1,), (1,)), ((), ())), preferred_element_type=F32)


def kernel(dims, nbr_ref, cnt_ref, box_ref, x_ref, axial_ref, rot_ref, out_map_ref, coup_ref, in_map_ref, tmat_ref,
           o_ref, cand, raw, flat_sums, box_rows, rows_own, rows_near, rows_other, w_pair, w_stack, scale, acc, sums, part, arrived, mom, mall, lhs_c, loc, ball, farbuf, maps,
           h_send, h_recv, f_send, f_recv, a_send, a_recv, m_send, m_recv, l_send, l_recv):
    ncell, ngrp, chunks, sd, slots, width, incid, lanes, nbc, pq = dims
    half = width // 2
    rows = nbc * pq
    pairs = slots // 2
    n = lax.axis_index("cells")
    g = lax.axis_index("grp")
    par = n % 2
    partner = n + 1 - 2 * par
    onward = n + 2 - 4 * par
    source = n - 2 + 4 * par
    forwards = jnp.logical_and(onward >= 0, onward < ncell)
    receives = jnp.logical_and(source >= 0, source < ncell)
    near_slot = 2 * (1 - par)
    other_slot = 2 * par
    group = sd * 2 // chunks
    flat = width * incid

    def cell(d):
        return lax.rem(n + d, ncell)

    def member(d):
        return lax.rem(g + d, ngrp)

    barrier = pltpu.get_barrier_semaphore()
    for d in range(1, ncell):
        pl.semaphore_signal(barrier, inc=1, device_id=(cell(d), g), device_id_type=MESH)
    for d in range(1, ngrp):
        pl.semaphore_signal(barrier, inc=1, device_id=(n, member(d)), device_id_type=MESH)
    pl.semaphore_wait(barrier, ncell + ngrp - 2)

    def piece(h):
        return pl.ds(h // 2 * group, group), pl.ds(h % 2 * (flat // 2), flat // 2)

    def swap(h):
        return pltpu.make_async_remote_copy(
            src_ref=x_ref.at[piece(h)], dst_ref=raw.at[(par,) + piece(h)],
            send_sem=h_send.at[h], recv_sem=h_recv.at[h], device_id=(partner, g), device_id_type=MESH)

    def forward(h):
        return pltpu.make_async_remote_copy(
            src_ref=raw.at[(1 - par,) + piece(h)], dst_ref=raw.at[(par,) + piece(h)],
            send_sem=f_send.at[h], recv_sem=f_recv.at[h], device_id=(onward, g), device_id_type=MESH)

    for h in range(chunks):
        swap(h).start()

    per = lanes // incid
    tiles = flat // lanes
    below = jnp.zeros((lanes - width, lanes), F32)

    def lay_rows(load, dst, r, span):
        for t in span:
            v = load(t)
            for i in range(per):
                dst[pl.ds(r * group * width + t * per + i, group, stride=width), :] = (
                    v if i == 0 else pltpu.roll(v, lanes - i * incid, 1))

    def turned_block(src, s):
        return jnp.concatenate([src[s * width:(s + 1) * width, :], below], axis=0).T[:incid]

    box_of = jnp.zeros((nbc, sd), jnp.int32)
    column = lax.broadcasted_iota(jnp.int32, (nbc, sd), 1)
    for s in range(sd):
        box_of = jnp.where(column == s, box_ref[s], box_of)
    onehot = (box_of == lax.broadcasted_iota(jnp.int32, (nbc, sd), 0)).astype(F32).astype(BF16)
    flat_sums[...] = jnp.dot(onehot, x_ref[...], preferred_element_type=F32)
    for r in range(nbc // group):
        lay_rows(lambda t: flat_sums[r * group:(r + 1) * group, t * lanes:(t + 1) * lanes], box_rows, r, range(tiles))
    for b in range(nbc):
        total = turned_block(box_rows, b)
        for q in range(ngrp):
            sums[q, b * pq:(b + 1) * pq, :] = total[q * pq:(q + 1) * pq]
    for q in range(ngrp):
        part[q] = sums[q].astype(BF16)

    def spread(d):
        return pltpu.make_async_remote_copy(
            src_ref=part.at[member(d)], dst_ref=arrived.at[d], send_sem=a_send.at[d], recv_sem=a_recv.at[d],
            device_id=(n, member(d)), device_id_type=MESH)

    for d in range(1, ngrp):
        spread(d).start()

    for r in range(sd // group):
        lay_rows(lambda t: x_ref[r * group:(r + 1) * group, t * lanes:(t + 1) * lanes].astype(F32),
                 rows_own, r, range(tiles))
    for s in range(sd):
        cand[sd + s] = turned_block(rows_own, s).astype(BF16)

    @pl.when(jnp.logical_not(receives))
    def _():
        cand[pl.ds(other_slot * sd, sd)] = jnp.zeros((sd, incid, lanes), BF16)

    for m, ref in enumerate((out_map_ref, in_map_ref)):
        maps[m] = jnp.zeros((lanes, lanes), BF16)
        maps[m, :width, :width] = ref[...]

    for d in range(1, ngrp):
        spread(d).wait_recv()
    total = sums[g]
    for d in range(1, ngrp):
        total = total + arrived[d].astype(F32)
    high = total.astype(BF16)
    low = (total - high.astype(F32)).astype(BF16)
    moment = (dot_nt(high, maps[0]) + dot_nt(low, maps[0])).astype(BF16)
    mom[...] = moment

    def share(d):
        return pltpu.make_async_remote_copy(
            src_ref=mom, dst_ref=mall.at[n], send_sem=m_send.at[d], recv_sem=m_recv.at[d],
            device_id=(cell(d), g), device_id_type=MESH)

    for d in range(1, ncell):
        share(d).start()
    mall[n] = moment

    for h in range(chunks):
        swap(h).wait_recv()

        @pl.when(forwards)
        def _():
            forward(h).start()

    w_pair[...] = jnp.zeros_like(w_pair)
    w_stack[...] = jnp.zeros_like(w_stack)
    scale[...] = jnp.zeros_like(scale)
    acc[...] = jnp.zeros_like(acc)

    @pl.loop(0, pairs)
    def _(j):
        for i in range(2):
            r = rot_ref[2 * j + i]
            w_pair[j, i * lanes:i * lanes + width, i * lanes:i * lanes + width] = r
            w_stack[j, i * lanes:i * lanes + width, :width] = r

    slot_id = lax.broadcasted_iota(jnp.int32, (slots, width), 0)
    for s in range(sd):
        live = jnp.where(slot_id < cnt_ref[s], 1.0, 0.0)
        scale[s, :, :width] = axial_ref[s].astype(F32) * live

    nbox = ncell * nbc
    row_box = lax.broadcasted_iota(jnp.int32, (rows, nbox), 0) // pq + n * nbc
    pick = (row_box == lax.broadcasted_iota(jnp.int32, (rows, nbox), 1)).astype(F32).astype(BF16)
    mine = jnp.dot(pick, coup_ref[...], preferred_element_type=F32).astype(BF16)
    for c in range(ncell):
        col_box = lax.broadcasted_iota(jnp.int32, (nbox, rows), 1) // pq + c * nbc
        put = (col_box == lax.broadcasted_iota(jnp.int32, (nbox, rows), 0)).astype(F32).astype(BF16)
        wide = jnp.dot(mine, put, preferred_element_type=F32)
        same = (lax.broadcasted_iota(jnp.int32, (rows, rows), 0) % pq
                == lax.broadcasted_iota(jnp.int32, (rows, rows), 1) % pq)
        lhs_c[c] = jnp.where(same, wide, 0.0).astype(BF16)

    def take(copy, slot, rows_of, place):
        for h in range(chunks):
            if copy is not None:
                copy(h).wait_recv()
            r = h // 2
            lay_rows(lambda t: raw[slot, r * group:(r + 1) * group, t * lanes:(t + 1) * lanes].astype(F32),
                     rows_of, r, range(h % 2 * (tiles // 2), (h % 2 + 1) * (tiles // 2)))
            if h % 2 == 1:
                for s in range(r * group, (r + 1) * group):
                    cand[place * sd + s] = turned_block(rows_of, s).astype(BF16)

    take(None, 1 - par, rows_near, near_slot)

    @pl.when(receives)
    def _():
        take(forward, par, rows_other, other_slot)

    block = 4

    def near(j):
        for sb in range(0, sd, block):
            lhs = jnp.concatenate([
                jnp.concatenate([cand[nbr_ref[s, 2 * j]], cand[nbr_ref[s, 2 * j + 1]]], axis=1)
                for s in range(sb, sb + block)], axis=0)
            turned = dot_nt(lhs, w_pair[j])
            scaled = jnp.concatenate([
                turned[(s - sb) * incid:(s - sb + 1) * incid]
                * jnp.concatenate([scale[s, pl.ds(2 * j, 1), :], scale[s, pl.ds(2 * j + 1, 1), :]], axis=1)
                for s in range(sb, sb + block)], axis=0).astype(BF16)
            acc[sb * incid:(sb + block) * incid, :] += jnp.dot(scaled, w_stack[j], preferred_element_type=F32)

    @pl.loop(0, pairs // 4)
    def _(j):
        near(2 * j)
        near(2 * j + 1)

    for d in range(1, ncell):
        share(d).wait_recv()
    local = jnp.zeros((rows, lanes), F32)
    for c in range(ncell):
        local = local + jnp.dot(lhs_c[c], mall[c], preferred_element_type=F32)
    local = local.astype(BF16)
    loc[...] = local

    def spread_local(d):
        return pltpu.make_async_remote_copy(
            src_ref=loc, dst_ref=ball.at[g], send_sem=l_send.at[d], recv_sem=l_recv.at[d],
            device_id=(n, member(d)), device_id_type=MESH)

    for d in range(1, ngrp):
        spread_local(d).start()
    ball[g] = local

    @pl.loop(pairs // 4, pairs // 2)
    def _(j):
        near(2 * j)
        near(2 * j + 1)

    for d in range(1, ngrp):
        spread_local(d).wait_recv()
    for q in range(ngrp):
        far = dot_nt(ball[q], maps[1])
        for b in range(nbc):
            farbuf[b, q * pq:(q + 1) * pq, :] = far[b * pq:(b + 1) * pq]

    lane = lax.broadcasted_iota(jnp.int32, (incid, lanes), 1)
    fill = jnp.zeros((sd, lanes - width), F32)
    real_t = tmat_ref[:, :half]
    imag_t = tmat_ref[:, half:]
    same_t = jnp.concatenate([real_t, real_t, fill], axis=1)
    swap_t = jnp.concatenate([-imag_t, imag_t, fill], axis=1)
    for s in range(sd):
        u = acc[s * incid:(s + 1) * incid, :] + farbuf[box_ref[s]]
        turned = jnp.where(lane < half, pltpu.roll(u, lanes - half, 1), pltpu.roll(u, half, 1))
        v = same_t[s:s + 1] * u + swap_t[s:s + 1] * turned
        own = (cand[sd + s].astype(F32) - v).astype(BF16).astype(F32)
        own = jnp.concatenate([own, jnp.zeros((lanes - incid, lanes), F32)], axis=0)
        rows_own[s * width:(s + 1) * width, :] = own.T[:width]
    for r in range(sd // group):
        for t in range(tiles):
            v = None
            for i in range(per):
                got = rows_own[pl.ds(r * group * width + t * per + i, group, stride=width), :]
                v = got if v is None else v + pltpu.roll(got, i * incid, 1)
            o_ref[r * group:(r + 1) * group, t * lanes:(t + 1) * lanes] = v.astype(BF16)

    for h in range(chunks):
        swap(h).wait_send()

    @pl.when(forwards)
    def _():
        for h in range(chunks):
            forward(h).wait_send()

    for d in range(1, ngrp):
        spread(d).wait_send()
        spread_local(d).wait_send()
    for d in range(1, ncell):
        share(d).wait_send()


def shards(ncell, ngrp, coeffs, neighbours, counts, boxes, axial, rotations, out_map, coupling, in_map, tmat):
    sd, slots = neighbours.shape
    width = rotations.shape[1]
    incid = coeffs.shape[1] // width
    lanes = -(-width // 128) * 128
    nbc = NBG * ngrp
    pq = incid // ngrp
    rows = nbc * pq
    chunks = sd // 8 * 2
    flat = width * incid
    pairs = slots // 2
    smem = pl.BlockSpec(memory_space=pltpu.SMEM)
    vmem = pl.BlockSpec(memory_space=pltpu.VMEM)
    dma = pltpu.SemaphoreType.DMA
    return pl.pallas_call(
        functools.partial(kernel, (ncell, ngrp, chunks, sd, slots, width, incid, lanes, nbc, pq)),
        out_shape=jax.ShapeDtypeStruct((sd, flat), BF16),
        in_specs=[smem] * 3 + [vmem] * 7,
        out_specs=vmem,
        scratch_shapes=[
            pltpu.VMEM((3 * sd, incid, lanes), BF16),
            pltpu.VMEM((2, sd, flat), BF16),
            pltpu.VMEM((nbc, flat), F32),
            pltpu.VMEM((nbc * width, lanes), F32),
            pltpu.VMEM((sd * width, lanes), F32),
            pltpu.VMEM((sd * width, lanes), F32),
            pltpu.VMEM((sd * width, lanes), F32),
            pltpu.VMEM((pairs, 2 * lanes, 2 * lanes), BF16),
            pltpu.VMEM((pairs, 2 * lanes, lanes), BF16),
            pltpu.VMEM((sd, slots, lanes), F32),
            pltpu.VMEM((sd * incid, lanes), F32),
            pltpu.VMEM((ngrp, rows, lanes), F32),
            pltpu.VMEM((ngrp, rows, lanes), BF16),
            pltpu.VMEM((ngrp, rows, lanes), BF16),
            pltpu.VMEM((rows, lanes), BF16),
            pltpu.VMEM((ncell, rows, lanes), BF16),
            pltpu.VMEM((ncell, rows, rows), BF16),
            pltpu.VMEM((rows, lanes), BF16),
            pltpu.VMEM((ngrp, rows, lanes), BF16),
            pltpu.VMEM((nbc, incid, lanes), F32),
            pltpu.VMEM((2, lanes, lanes), BF16),
            dma((chunks,)), dma((chunks,)), dma((chunks,)), dma((chunks,)),
            dma((ngrp,)), dma((ngrp,)), dma((ncell,)), dma((ncell,)), dma((ngrp,)), dma((ngrp,)),
        ],
        compiler_params=pltpu.CompilerParams(collective_id=0, has_side_effects=True),
    )(neighbours, counts, boxes, coeffs, axial, rotations, out_map, coupling, in_map, tmat)


def solution(mesh):
    in_specs = (
        P(("cells", "grp"), None),
        P(("cells", "grp"), None),
        P(("cells", "grp")),
        P(("cells", "grp")),
        P(("cells", "grp"), None, None),
        P(),
        P(),
        P(),
        P(),
        P(("cells", "grp"), None),
    )
    out_specs = P(("cells", "grp"), None)
    body = functools.partial(shards, mesh.shape["cells"], mesh.shape["grp"])
    return jax.shard_map(body, mesh=mesh, in_specs=in_specs, out_specs=out_specs, check_vma=False)
```

```python
import functools

import jax
import jax.numpy as jnp
from jax import lax
from jax.experimental import pallas as pl
from jax.experimental.pallas import tpu as pltpu
from jax.sharding import PartitionSpec as P

NBG = 2
MESH = pl.DeviceIdType.MESH
F32 = jnp.float32
BF16 = jnp.bfloat16


def dot_nt(a, b):
    return lax.dot_general(a, b, (((1,), (1,)), ((), ())), preferred_element_type=F32)


def kernel(dims, nbr_ref, cnt_ref, box_ref, x_ref, axial_ref, rot_ref, out_map_ref, coup_ref, in_map_ref, tmat_ref,
           o_ref, cand, raw, flat_sums, box_rows, rows_own, rows_near, rows_other, w_pair, w_stack, scale, acc, sums, part, arrived, mom, mall, lhs_c, loc, ball, farbuf, maps,
           h_send, h_recv, f_send, f_recv, a_send, a_recv, m_send, m_recv, l_send, l_recv, g_send, g_recv, giving, given):
    ncell, ngrp, chunks, sd, slots, width, incid, lanes, nbc, pq = dims
    half = width // 2
    rows = nbc * pq
    pairs = slots // 2
    n = lax.axis_index("cells")
    g = lax.axis_index("grp")
    par = n % 2
    partner = n + 1 - 2 * par
    onward = n + 2 - 4 * par
    source = n - 2 + 4 * par
    forwards = jnp.logical_and(onward >= 0, onward < ncell)
    receives = jnp.logical_and(source >= 0, source < ncell)
    near_slot = 2 * (1 - par)
    other_slot = 2 * par
    group = sd * 2 // chunks
    flat = width * incid

    nhalf = ncell // 2
    mine_at = n // 2

    def cell(d):
        return par + 2 * lax.rem(mine_at + d, nhalf)

    def member(d):
        return lax.rem(g + d, ngrp)

    barrier = pltpu.get_barrier_semaphore()
    for d in range(1, nhalf):
        pl.semaphore_signal(barrier, inc=1, device_id=(cell(d), g), device_id_type=MESH)
    pl.semaphore_signal(barrier, inc=1, device_id=(partner, g), device_id_type=MESH)
    for d in range(1, ngrp):
        pl.semaphore_signal(barrier, inc=1, device_id=(n, member(d)), device_id_type=MESH)
    pl.semaphore_wait(barrier, nhalf + ngrp - 1)

    def piece(h):
        return pl.ds(h // 2 * group, group), pl.ds(h % 2 * (flat // 2), flat // 2)

    def swap(h):
        return pltpu.make_async_remote_copy(
            src_ref=x_ref.at[piece(h)], dst_ref=raw.at[(par,) + piece(h)],
            send_sem=h_send.at[h], recv_sem=h_recv.at[h], device_id=(partner, g), device_id_type=MESH)

    def forward(h):
        return pltpu.make_async_remote_copy(
            src_ref=raw.at[(1 - par,) + piece(h)], dst_ref=raw.at[(par,) + piece(h)],
            send_sem=f_send.at[h], recv_sem=f_recv.at[h], device_id=(onward, g), device_id_type=MESH)

    for h in range(chunks):
        swap(h).start()

    per = lanes // incid
    tiles = flat // lanes
    below = jnp.zeros((lanes - width, lanes), F32)

    def lay_rows(load, dst, r, span):
        for t in span:
            v = load(t)
            for i in range(per):
                dst[pl.ds(r * group * width + t * per + i, group, stride=width), :] = (
                    v if i == 0 else pltpu.roll(v, lanes - i * incid, 1))

    def turned_block(src, s):
        return jnp.concatenate([src[s * width:(s + 1) * width, :], below], axis=0).T[:incid]

    box_of = jnp.zeros((nbc, sd), jnp.int32)
    column = lax.broadcasted_iota(jnp.int32, (nbc, sd), 1)
    for s in range(sd):
        box_of = jnp.where(column == s, box_ref[s], box_of)
    onehot = (box_of == lax.broadcasted_iota(jnp.int32, (nbc, sd), 0)).astype(F32).astype(BF16)
    flat_sums[...] = jnp.dot(onehot, x_ref[...], preferred_element_type=F32)
    for r in range(nbc // group):
        lay_rows(lambda t: flat_sums[r * group:(r + 1) * group, t * lanes:(t + 1) * lanes], box_rows, r, range(tiles))
    for b in range(nbc):
        total = turned_block(box_rows, b)
        for q in range(ngrp):
            sums[q, b * pq:(b + 1) * pq, :] = total[q * pq:(q + 1) * pq]
    for q in range(ngrp):
        part[q] = sums[q].astype(BF16)

    def spread(d):
        return pltpu.make_async_remote_copy(
            src_ref=part.at[member(d)], dst_ref=arrived.at[d], send_sem=a_send.at[d], recv_sem=a_recv.at[d],
            device_id=(n, member(d)), device_id_type=MESH)

    for d in range(1, ngrp):
        spread(d).start()

    for r in range(sd // group):
        lay_rows(lambda t: x_ref[r * group:(r + 1) * group, t * lanes:(t + 1) * lanes].astype(F32),
                 rows_own, r, range(tiles))
    for s in range(sd):
        cand[sd + s] = turned_block(rows_own, s).astype(BF16)

    @pl.when(jnp.logical_not(receives))
    def _():
        cand[pl.ds(other_slot * sd, sd)] = jnp.zeros((sd, incid, lanes), BF16)

    for m, ref in enumerate((out_map_ref, in_map_ref)):
        maps[m] = jnp.zeros((lanes, lanes), BF16)
        maps[m, :width, :width] = ref[...]

    for h in range(chunks // 2):
        swap(h).wait_recv()

        @pl.when(forwards)
        def _():
            forward(h).start()

    for d in range(1, ngrp):
        spread(d).wait_recv()
    total = sums[g]
    for d in range(1, ngrp):
        total = total + arrived[d].astype(F32)
    high = total.astype(BF16)
    low = (total - high.astype(F32)).astype(BF16)
    moment = (dot_nt(high, maps[0]) + dot_nt(low, maps[0])).astype(BF16)
    mom[...] = moment

    def share(d):
        return pltpu.make_async_remote_copy(
            src_ref=mom, dst_ref=mall.at[mine_at], send_sem=m_send.at[d], recv_sem=m_recv.at[d],
            device_id=(cell(d), g), device_id_type=MESH)

    for d in range(1, nhalf):
        share(d).start()
    mall[mine_at] = moment

    for h in range(chunks // 2, chunks):
        swap(h).wait_recv()

        @pl.when(forwards)
        def _():
            forward(h).start()

    w_pair[...] = jnp.zeros_like(w_pair)
    w_stack[...] = jnp.zeros_like(w_stack)
    scale[...] = jnp.zeros_like(scale)
    acc[...] = jnp.zeros_like(acc)

    @pl.loop(0, pairs)
    def _(j):
        for i in range(2):
            r = rot_ref[2 * j + i]
            w_pair[j, i * lanes:i * lanes + width, i * lanes:i * lanes + width] = r
            w_stack[j, i * lanes:i * lanes + width, :width] = r

    slot_id = lax.broadcasted_iota(jnp.int32, (slots, width), 0)
    for s in range(sd):
        live = jnp.where(slot_id < cnt_ref[s], 1.0, 0.0)
        scale[s, :, :width] = axial_ref[s].astype(F32) * live

    nbox = ncell * nbc
    same = (lax.broadcasted_iota(jnp.int32, (rows, rows), 0) % pq
            == lax.broadcasted_iota(jnp.int32, (rows, rows), 1) % pq)
    for k, target in enumerate((n, partner)):
        row_box = lax.broadcasted_iota(jnp.int32, (rows, nbox), 0) // pq + target * nbc
        pick = (row_box == lax.broadcasted_iota(jnp.int32, (rows, nbox), 1)).astype(F32).astype(BF16)
        chosen = jnp.dot(pick, coup_ref[...], preferred_element_type=F32).astype(BF16)
        for m in range(nhalf):
            col_box = lax.broadcasted_iota(jnp.int32, (nbox, rows), 1) // pq + (par + 2 * m) * nbc
            put = (col_box == lax.broadcasted_iota(jnp.int32, (nbox, rows), 0)).astype(F32).astype(BF16)
            wide = jnp.dot(chosen, put, preferred_element_type=F32)
            lhs_c[k, m] = jnp.where(same, wide, 0.0).astype(BF16)

    def take(copy, slot, rows_of, place):
        for h in range(chunks):
            if copy is not None:
                copy(h).wait_recv()
            r = h // 2
            lay_rows(lambda t: raw[slot, r * group:(r + 1) * group, t * lanes:(t + 1) * lanes].astype(F32),
                     rows_of, r, range(h % 2 * (tiles // 2), (h % 2 + 1) * (tiles // 2)))
            if h % 2 == 1:
                for s in range(r * group, (r + 1) * group):
                    cand[place * sd + s] = turned_block(rows_of, s).astype(BF16)

    take(None, 1 - par, rows_near, near_slot)

    def give():
        return pltpu.make_async_remote_copy(
            src_ref=giving, dst_ref=given, send_sem=g_send, recv_sem=g_recv,
            device_id=(partner, g), device_id_type=MESH)

    for d in range(1, nhalf):
        share(d).wait_recv()
    partial = jnp.dot(lhs_c[1, 0], mall[0], preferred_element_type=F32)
    for m in range(1, nhalf):
        partial = partial + jnp.dot(lhs_c[1, m], mall[m], preferred_element_type=F32)
    giving[...] = partial
    give().start()

    @pl.when(receives)
    def _():
        take(forward, par, rows_other, other_slot)

    block = 4

    def near(j):
        for sb in range(0, sd, block):
            lhs = jnp.concatenate([
                jnp.concatenate([cand[nbr_ref[s, 2 * j]], cand[nbr_ref[s, 2 * j + 1]]], axis=1)
                for s in range(sb, sb + block)], axis=0)
            turned = dot_nt(lhs, w_pair[j])
            scaled = jnp.concatenate([
                turned[(s - sb) * incid:(s - sb + 1) * incid]
                * jnp.concatenate([scale[s, pl.ds(2 * j, 1), :], scale[s, pl.ds(2 * j + 1, 1), :]], axis=1)
                for s in range(sb, sb + block)], axis=0).astype(BF16)
            acc[sb * incid:(sb + block) * incid, :] += jnp.dot(scaled, w_stack[j], preferred_element_type=F32)

    @pl.loop(0, pairs // 16)
    def _(j):
        for i in range(8):
            near(8 * j + i)

    give().wait_recv()
    local = given[...]
    for m in range(nhalf):
        local = local + jnp.dot(lhs_c[0, m], mall[m], preferred_element_type=F32)
    local = local.astype(BF16)
    loc[...] = local

    def spread_local(d):
        return pltpu.make_async_remote_copy(
            src_ref=loc, dst_ref=ball.at[g], send_sem=l_send.at[d], recv_sem=l_recv.at[d],
            device_id=(n, member(d)), device_id_type=MESH)

    for d in range(1, ngrp):
        spread_local(d).start()
    ball[g] = local

    @pl.loop(pairs // 16, pairs // 8)
    def _(j):
        for i in range(8):
            near(8 * j + i)

    for d in range(1, ngrp):
        spread_local(d).wait_recv()
    for q in range(ngrp):
        far = dot_nt(ball[q], maps[1])
        for b in range(nbc):
            farbuf[b, q * pq:(q + 1) * pq, :] = far[b * pq:(b + 1) * pq]

    lane = lax.broadcasted_iota(jnp.int32, (incid, lanes), 1)
    fill = jnp.zeros((sd, lanes - width), F32)
    real_t = tmat_ref[:, :half]
    imag_t = tmat_ref[:, half:]
    same_t = jnp.concatenate([real_t, real_t, fill], axis=1)
    swap_t = jnp.concatenate([-imag_t, imag_t, fill], axis=1)
    for s in range(sd):
        u = acc[s * incid:(s + 1) * incid, :] + farbuf[box_ref[s]]
        turned = jnp.where(lane < half, pltpu.roll(u, lanes - half, 1), pltpu.roll(u, half, 1))
        v = same_t[s:s + 1] * u + swap_t[s:s + 1] * turned
        own = (cand[sd + s].astype(F32) - v).astype(BF16).astype(F32)
        own = jnp.concatenate([own, jnp.zeros((lanes - incid, lanes), F32)], axis=0)
        rows_own[s * width:(s + 1) * width, :] = own.T[:width]
    for r in range(sd // group):
        for t in range(tiles):
            v = None
            for i in range(per):
                got = rows_own[pl.ds(r * group * width + t * per + i, group, stride=width), :]
                v = got if v is None else v + pltpu.roll(got, i * incid, 1)
            o_ref[r * group:(r + 1) * group, t * lanes:(t + 1) * lanes] = v.astype(BF16)

    for h in range(chunks):
        swap(h).wait_send()

    @pl.when(forwards)
    def _():
        for h in range(chunks):
            forward(h).wait_send()

    for d in range(1, ngrp):
        spread(d).wait_send()
        spread_local(d).wait_send()
    for d in range(1, nhalf):
        share(d).wait_send()
    give().wait_send()


def shards(ncell, ngrp, coeffs, neighbours, counts, boxes, axial, rotations, out_map, coupling, in_map, tmat):
    sd, slots = neighbours.shape
    width = rotations.shape[1]
    incid = coeffs.shape[1] // width
    lanes = -(-width // 128) * 128
    nbc = NBG * ngrp
    pq = incid // ngrp
    rows = nbc * pq
    chunks = sd // 8 * 2
    flat = width * incid
    pairs = slots // 2
    smem = pl.BlockSpec(memory_space=pltpu.SMEM)
    vmem = pl.BlockSpec(memory_space=pltpu.VMEM)
    dma = pltpu.SemaphoreType.DMA
    return pl.pallas_call(
        functools.partial(kernel, (ncell, ngrp, chunks, sd, slots, width, incid, lanes, nbc, pq)),
        out_shape=jax.ShapeDtypeStruct((sd, flat), BF16),
        in_specs=[smem] * 3 + [vmem] * 7,
        out_specs=vmem,
        scratch_shapes=[
            pltpu.VMEM((3 * sd, incid, lanes), BF16),
            pltpu.VMEM((2, sd, flat), BF16),
            pltpu.VMEM((nbc, flat), F32),
            pltpu.VMEM((nbc * width, lanes), F32),
            pltpu.VMEM((sd * width, lanes), F32),
            pltpu.VMEM((sd * width, lanes), F32),
            pltpu.VMEM((sd * width, lanes), F32),
            pltpu.VMEM((pairs, 2 * lanes, 2 * lanes), BF16),
            pltpu.VMEM((pairs, 2 * lanes, lanes), BF16),
            pltpu.VMEM((sd, slots, lanes), F32),
            pltpu.VMEM((sd * incid, lanes), F32),
            pltpu.VMEM((ngrp, rows, lanes), F32),
            pltpu.VMEM((ngrp, rows, lanes), BF16),
            pltpu.VMEM((ngrp, rows, lanes), BF16),
            pltpu.VMEM((rows, lanes), BF16),
            pltpu.VMEM((ncell // 2, rows, lanes), BF16),
            pltpu.VMEM((2, ncell // 2, rows, rows), BF16),
            pltpu.VMEM((rows, lanes), BF16),
            pltpu.VMEM((ngrp, rows, lanes), BF16),
            pltpu.VMEM((nbc, incid, lanes), F32),
            pltpu.VMEM((2, lanes, lanes), BF16),
            dma((chunks,)), dma((chunks,)), dma((chunks,)), dma((chunks,)),
            dma((ngrp,)), dma((ngrp,)), dma((ncell,)), dma((ncell,)), dma((ngrp,)), dma((ngrp,)), dma, dma,
            pltpu.VMEM((rows, lanes), F32),
            pltpu.VMEM((rows, lanes), F32),
        ],
        compiler_params=pltpu.CompilerParams(collective_id=0, has_side_effects=True),
    )(neighbours, counts, boxes, coeffs, axial, rotations, out_map, coupling, in_map, tmat)


def solution(mesh):
    in_specs = (
        P(("cells", "grp"), None),
        P(("cells", "grp"), None),
        P(("cells", "grp")),
        P(("cells", "grp")),
        P(("cells", "grp"), None, None),
        P(),
        P(),
        P(),
        P(),
        P(("cells", "grp"), None),
    )
    out_specs = P(("cells", "grp"), None)
    body = functools.partial(shards, mesh.shape["cells"], mesh.shape["grp"])
    return jax.shard_map(body, mesh=mesh, in_specs=in_specs, out_specs=out_specs, check_vma=False)
```
